256 devices in a mesh: row: 8 (over x_lo, y), col: 32 (over z, x_hi, core).
Axes of the slice: x: 4 (x_hi: 2, x_lo: 2; x = x_hi * 2 + x_lo), y: 4, z: 8, core: 2. Of those that a mesh axis runs over, the one named last changes fastest.
Arguments:
- sigma_anc: bfloat16 [32, 640, 20480], P(None, 'col', 'row'), may hold values from -6 to 6
- owner: int32 [32], replicated, may hold values from 0 to 31, as said below
- structure: int32 [32, 8], replicated, may hold values from 0 to 31, as said below
- factor: bfloat16 [32, 5120, 640], P('col', 'row'), may hold values from -0.078125 to 0.078125
- diag_inv: float32 [32, 640, 640], P('col', None, 'row'), may hold values from -6 to 6
Outputs:
- offdiag: bfloat16 [32, 5120, 640], P('col', 'row')
- diagblock: float32 [32, 640, 640], P('col', None, 'row')
The draws below stay inside these ranges and needn't reach their ends.
Inputs may be any that keep to these rules, and one draw needn't show every extreme that they name: owner maps each group of 4 ancestors, j // 4 equal, one to one onto the stored columns of the same group. `structure`: entry a of every supernode's list lies between a * 4 and (a + 1) * 4 - 1.
All inputs are finite; a program needn't handle non-finite values.
Results may differ from the reference program's by a relative error of at most 0.014.
Values may be sent and summed in bfloat16 or wider, within the bound.
No kernel may reach another device: no remote copies, remote signals or barrier semaphores. Data moves between devices by JAX's collectives and lax.ppermute only.
A program may use at most 64 MiB of HBM per device.

```python
import jax
import jax.numpy as jnp
from jax import lax

B = 640
NA = 32
GROUP = 4
S = 8
NS = 32


def draw_owner(key, part):
    group_keys = jax.random.split(jax.random.fold_in(key, 11), NA // GROUP)
    shuffled = jax.vmap(lambda single: jax.random.permutation(single, GROUP))(group_keys)
    starts = lax.broadcasted_iota(jnp.int32, (NA // GROUP, GROUP), 0) * GROUP
    return (shuffled.astype(jnp.int32) + starts).reshape(NA).astype(jnp.int32)


def draw_structure(key, part):
    key_one, key_two = jax.random.split(jax.random.fold_in(key, 7))
    first_pick = jax.random.randint(key_one, (NS, S), 0, GROUP)
    second_pick = jax.random.randint(key_two, (NS, S), 0, GROUP)
    offset = jnp.minimum(first_pick, second_pick)
    row_ids = lax.broadcasted_iota(jnp.int32, (NS, S), 0)
    slot_ids = lax.broadcasted_iota(jnp.int32, (NS, S), 1)
    offset = jnp.where((row_ids == NS - 1) & (slot_ids == S - 1), GROUP - 1, offset)
    offset = jnp.where((row_ids == 0) & (slot_ids == 0), 0, offset)
    return (slot_ids * GROUP + offset).astype(jnp.int32)


def level_of(rng, dims, pieces, low, high):
    gain, own = 1.0, jax.random.fold_in(rng, 6)
    for position, parts in pieces:
        draws = jnp.exp(jax.random.uniform(jax.random.fold_in(own, position), (parts,), jnp.float32, low / len(pieces), high / len(pieces)))
        gain = gain * jnp.repeat(draws, dims[position] // parts).reshape([-1 if axis == position else 1 for axis in range(len(dims))])
    return gain


def gaussian(key, shape, scale, reach, pieces=(), held_as=jnp.bfloat16):
    result = scale * jax.random.normal(key, shape, jnp.float32)
    if pieces:
        result = result * level_of(key, shape, pieces, -0.22, 0.18)
    return jnp.clip(result, -reach, reach).astype(held_as)


def setup_inputs(seed: int = 0) -> dict:
    splits = jax.random.split(jax.random.key(seed), 6)
    return {
        "sigma_anc": gaussian(splits[0], (NA, B, NA * B), 1.0, 6.0, ((1, 32), (2, 8))),
        "owner": draw_owner(jax.random.fold_in(splits[5], 71), 0),
        "structure": draw_structure(jax.random.fold_in(splits[5], 71), 0),
        "factor": gaussian(splits[3], (NS, S * B, B), (S * B) ** -0.5, 0.078125, ((0, 32), (1, 8))),
        "diag_inv": gaussian(splits[4], (NS, B, B), 1.0, 6.0, ((0, 32), (2, 8)), jnp.float32),
    }


def reference(sigma_anc, owner, structure, factor, diag_inv):
    blocks = sigma_anc.reshape(NA, B, NA, B)

    def per_supernode(inputs):
        listed, factor_panel, inverse_diag = inputs
        stored = jnp.take(owner, listed)
        picked = jnp.take(blocks, stored, axis=2)
        picked = jnp.take(picked, listed, axis=0)
        panel_blocks = factor_panel.reshape(S, B, B).astype(jnp.float32)
        slot_terms = jnp.einsum('aibj,bjk->baik', picked.astype(jnp.float32), panel_blocks)
        slot_terms = lax.optimization_barrier(slot_terms.astype(jnp.bfloat16)).astype(jnp.float32)
        offdiag = (-jnp.sum(slot_terms, axis=0)).reshape(S * B, B).astype(jnp.bfloat16)
        products = lax.dot_general(factor_panel, offdiag, (((0,), (0,)), ((), ())), preferred_element_type=jnp.float32)
        return offdiag, inverse_diag - products

    offdiag, diagblock = lax.map(per_supernode, (structure, factor, diag_inv))
    return offdiag, diagblock
```

```python
import functools

import jax
import jax.numpy as jnp
from jax import lax
from jax.experimental import pallas as pl
from jax.experimental.pallas import tpu as pltpu
from jax.sharding import PartitionSpec as P


NZ, NQ, NY, NX = 8, 4, 4, 2
SLOTS = 8
GROUP = 4
CHUNKS = ((0, 1, 7), (2, 6), (3, 5, 4))


def shift_z(step):
    return [(z * NQ + q, (z + step) % NZ * NQ + q) for z in range(NZ) for q in range(NQ)]


def flip_q(mask):
    return [(z * NQ + q, z * NQ + (q ^ mask)) for z in range(NZ) for q in range(NQ)]


def shift_y(step):
    return [(x * NY + y, x * NY + (y + step) % NY) for x in range(NX) for y in range(NY)]


FLIP_X = [(x * NY + y, (1 - x) * NY + y) for x in range(NX) for y in range(NY)]


def gather_kernel(offsets, pos, structure, owner, sigma, o0, o1, o2, o3, wide):
    rows, width = sigma.shape[1], o0.shape[2]
    b, z, q = pos[0], pos[1], pos[2]
    for n, offset in enumerate(offsets):
        for e, out in enumerate((o0, o1, o2, o3)):
            k = ((z + offset) & (NZ - 1)) * NQ + (q ^ e)
            column = pl.multiple_of((owner[structure[k, b]] - b * GROUP) * width, width)
            for s in range(SLOTS):
                a = ((b >> 2) ^ (s >> 2)) * NY + ((b + s) & (NY - 1))
                block = sigma[structure[k, a], :, pl.ds(column, width)]
                wide[s * rows:(s + 1) * rows, :] = block.astype(jnp.float32)
            out[n] = wide[...].astype(jnp.bfloat16)


def gather_blocks(offsets, pos, structure, owner, sigma, width):
    rows = SLOTS * sigma.shape[1]
    shape = jax.ShapeDtypeStruct((len(offsets), rows, width), jnp.bfloat16)
    smem = pl.BlockSpec(memory_space=pltpu.SMEM)
    vmem = pl.BlockSpec(memory_space=pltpu.VMEM)
    return pl.pallas_call(
        functools.partial(gather_kernel, offsets),
        out_shape=(shape,) * NQ,
        in_specs=[smem, smem, smem, vmem],
        out_specs=(vmem,) * NQ,
        scratch_shapes=[pltpu.VMEM((rows, width), jnp.float32)],
        name="gather_blocks",
    )(pos, structure, owner, sigma)


def term_kernel(count, pieces, pos, *refs):
    lefts = refs[:NQ]
    factors = refs[NQ:NQ + sum(pieces)]
    outs = refs[NQ + sum(pieces):NQ + sum(pieces) + NY]
    left, wide, stage = refs[-3:]
    block, width = left.shape[1], left.shape[2]
    rows = block // SLOTS
    q = pos[2]
    at = 0
    for n in range(count):
        for e in range(NQ):
            left[q ^ e] = lefts[e][n]
        held = [ref[...] for ref in factors[at:at + pieces[n]]]
        at += pieces[n]
        right = held[0] if len(held) == 1 else jnp.concatenate(held, axis=0)
        wide[...] = jnp.dot(left[...].reshape(NQ * block, width), right, preferred_element_type=jnp.float32)
        for s in range(SLOTS):
            for e in range(NQ):
                start = e * block + s * rows
                stage[e * rows:(e + 1) * rows, :] = wide[start:start + rows, :]
            outs[s & (NY - 1)][s >> 2, n] = stage[...].astype(jnp.bfloat16)


def slot_terms(pos, lefts, factors):
    count, block, width = lefts[0].shape
    pieces = tuple(len(f) for f in factors)
    flat = [piece for f in factors for piece in f]
    shape = jax.ShapeDtypeStruct((NX, count, NQ * block // SLOTS, width), jnp.bfloat16)
    smem = pl.BlockSpec(memory_space=pltpu.SMEM)
    vmem = pl.BlockSpec(memory_space=pltpu.VMEM)
    return pl.pallas_call(
        functools.partial(term_kernel, count, pieces),
        out_shape=(shape,) * NY,
        in_specs=[smem] + [vmem] * (NQ + len(flat)),
        out_specs=(vmem,) * NY,
        scratch_shapes=[
            pltpu.VMEM((NQ, block, width), jnp.bfloat16),
            pltpu.VMEM((NQ * block, width), jnp.float32),
            pltpu.VMEM((NQ * block // SLOTS, width), jnp.float32),
        ],
        name="slot_terms",
    )(pos, *lefts, *flat)


def finish_kernel(pos, *refs):
    pieces, factor, off, part = refs[:NZ], refs[NZ], refs[NZ + 1], refs[NZ + 2]
    z = pos[1]
    for s in range(NZ):
        off[(z - s) & (NZ - 1)] = pieces[s][...]
    whole = off[...].reshape(factor.shape)
    product = lax.dot_general(whole, factor[...], (((0,), (0,)), ((), ())), preferred_element_type=jnp.float32)
    part[...] = product.astype(jnp.bfloat16).reshape(part.shape)


def finish(pos, pieces, factor):
    rows, width = pieces[0].shape
    smem = pl.BlockSpec(memory_space=pltpu.SMEM)
    vmem = pl.BlockSpec(memory_space=pltpu.VMEM)
    return pl.pallas_call(
        finish_kernel,
        out_shape=(
            jax.ShapeDtypeStruct((NZ, rows, width), jnp.bfloat16),
            jax.ShapeDtypeStruct((NX * NY, width // (NX * NY), width), jnp.bfloat16),
        ),
        in_specs=[smem] + [vmem] * (NZ + 1),
        out_specs=(vmem, vmem),
        name="finish",
    )(pos, *pieces, factor)


def body(sigma_anc, owner, structure, factor, diag_inv):
    here_row, here_col = lax.axis_index("row"), lax.axis_index("col")
    pos = jnp.stack([here_row, here_col // NQ, here_col % NQ]).astype(jnp.int32)
    own = factor[0]
    width = own.shape[1]
    half = width // 2

    held = {0: (own,)}
    right, left = own, own
    for s in range(1, NZ // 2):
        right = lax.ppermute(right, "col", shift_z(-1))
        left = lax.ppermute(left, "col", shift_z(1))
        held[s], held[NZ - s] = (right,), (left,)
    held[NZ // 2] = (
        lax.ppermute(right[:half], "col", shift_z(-1)),
        lax.ppermute(left[half:], "col", shift_z(1)),
    )

    finished = {}
    for offsets in CHUNKS:
        sent = gather_blocks(offsets, pos, structure, owner, sigma_anc, width)
        lefts = [sent[0]] + [lax.ppermute(sent[e], "col", flip_q(e)) for e in range(1, NQ)]
        terms = slot_terms(pos, lefts, [held[s] for s in offsets])
        total = terms[0].astype(jnp.float32)
        for d in range(1, NY):
            total = total + lax.ppermute(terms[d], "row", shift_y(d)).astype(jnp.float32)
        other = lax.ppermute(total[1].astype(jnp.bfloat16), "row", FLIP_X)
        rows = -(total[0] + other.astype(jnp.float32))
        for n, s in enumerate(offsets):
            piece = rows[n].astype(jnp.bfloat16)
            finished[s] = piece if s == 0 else lax.ppermute(piece, "col", shift_z(s))

    offdiag, parts = finish(pos, [finished[s] for s in range(NZ)], own)
    parts = lax.all_to_all(parts, "row", split_axis=0, concat_axis=0, tiled=True)
    diagonal = jnp.sum(parts.astype(jnp.float32), axis=0).T
    return offdiag.reshape(factor.shape), diag_inv - diagonal[None]


def solution(mesh):
    return jax.shard_map(
        body,
        mesh=mesh,
        in_specs=(P(None, "col", "row"), P(), P(), P("col", "row", None), P("col", None, "row")),
        out_specs=(P("col", "row", None), P("col", None, "row")),
        check_vma=False,
    )
```
